32 devices in a mesh: dp: 4 (over y, x), tensor: 8 (over z, core).
Axes of the slice: x: 2, y: 2, z: 4, core: 2. Of those that a mesh axis runs over, the one named last changes fastest.
Arguments:
- normed_input: bfloat16 [4096, 8192], P('dp', 'tensor'), may hold values from -6 to 6
- positions: int32 [4096], P('dp'), may hold values from 0 to 4095
- fixed_weight_matrix: bfloat16 [8192, 10240], P('dp', 'tensor'), may hold values from -0.09375 to 0.09375
- adapter_down_map: bfloat16 [8192, 16], P('tensor'), may hold values from -0.0625 to 0.0625
- adapter_up_map: bfloat16 [16, 10240], P(None, 'tensor'), may hold values from -0.0625 to 0.0625
- output_gradient: bfloat16 [4096, 10240], P('dp', 'tensor'), may hold values from -6 to 6
Outputs:
- grad_x: bfloat16 [4096, 8192], P('dp', 'tensor')
- grad_a: float32 [8192, 16], P('tensor')
- grad_b: float32 [16, 10240], P(None, 'tensor')
The draws below stay inside these ranges and needn't reach their ends.
All inputs are finite; a program needn't handle non-finite values.
Results may differ from the reference program's by a relative error of at most 0.0048.
Values may be sent and summed in bfloat16 or wider, within the bound.
A program may use at most 256 MiB of HBM per device.

```python
import jax
import jax.numpy as jnp

MODEL_WIDTH = 8192
KV = 1024
HEAD = 128
ADAPTER_RANK = 16
PROJECTION_COLS = 10240
TOKENS = 4096
N_TENSOR = 8


def place_ends(entries, stream_key, low, largest):
    index_at = [jax.random.randint(jax.random.fold_in(stream_key, axis), (), 0, length) for axis, length in enumerate(entries.shape)]
    longest = entries.shape.index(max(entries.shape))
    neighbour = index_at[:longest] + [(index_at[longest] + 1) % entries.shape[longest]] + index_at[longest + 1:]
    return entries.at[tuple(index_at)].set(low).at[tuple(neighbour)].set(largest)


def strengthened(array, rng, source, target, blocks, factor):
    owner, partner = [(jnp.arange(array.shape[dim]) // (array.shape[dim] // blocks)).reshape([-1 if axis == dim else 1 for axis in range(array.ndim)]) for dim in (source, target)]
    chosen = jax.random.permutation(rng, blocks)[partner]
    strong = (owner == chosen) | (owner == (partner + blocks // 2) % blocks)
    return jnp.where(strong, factor * array, array)


def shard_levels(key, extent, split, low, high):
    gain = 1.0
    for position, shards_of in split:
        heights = jax.random.uniform(jax.random.fold_in(jax.random.fold_in(key, 6), position), (shards_of,), jnp.float32, low / len(split), high / len(split))
        gain = gain * jnp.repeat(jnp.exp(heights), extent[position] // shards_of).reshape((-1,) + (1,) * (len(extent) - 1 - position))
    return gain


def gaussian(rng, dims, deviation, bound, pieces=(), kind=jnp.bfloat16):
    values = deviation * jax.random.normal(rng, dims, jnp.float32)
    if pieces:
        values = values * shard_levels(rng, dims, pieces, -0.22, 0.18)
    return jnp.clip(values, -bound, bound).astype(kind)


def noise_with(key, extent, scale, most, pieces, heavy, kind=jnp.bfloat16):
    entries = scale * jax.random.normal(key, extent, jnp.float32)
    if pieces:
        entries = entries * shard_levels(key, extent, pieces, -0.22, 0.18)
    return jnp.clip(strengthened(entries, jax.random.fold_in(key, 3), *heavy), -most, most).astype(kind)


def setup_inputs(seed: int = 0) -> dict:
    streams_of = jax.random.split(jax.random.key(seed), 7)
    return {
        "normed_input": gaussian(streams_of[0], (TOKENS, MODEL_WIDTH), 1.0, 6.0, ((0, 4), (1, 8))),
        "positions": place_ends(jax.random.randint(streams_of[1], (TOKENS,), 0, TOKENS), jax.random.fold_in(streams_of[1], 1), 0, TOKENS - 1).astype(jnp.int32),
        "fixed_weight_matrix": noise_with(streams_of[2], (MODEL_WIDTH, PROJECTION_COLS), MODEL_WIDTH ** -0.5, 0.09375, ((0, 4), (1, 8)), (1, 0, 8, 2.0)),
        "adapter_down_map": gaussian(streams_of[3], (MODEL_WIDTH, ADAPTER_RANK), MODEL_WIDTH ** -0.5, 0.0625, ((0, 8),)),
        "adapter_up_map": gaussian(streams_of[4], (ADAPTER_RANK, PROJECTION_COLS), PROJECTION_COLS ** -0.5, 0.0625, ((1, 8),)),
        "output_gradient": gaussian(streams_of[5], (TOKENS, PROJECTION_COLS), 1.0, 6.0, ((0, 4), (1, 8))),
    }


def rope_tables(positions, qkv):
    width = qkv // N_TENSOR
    q_width = MODEL_WIDTH // N_TENSOR
    k_width = KV // N_TENSOR
    column = jnp.arange(qkv, dtype=jnp.int32)
    block = column // width
    offset = column % width
    is_query = offset < q_width
    is_key = jnp.logical_and(offset >= q_width, offset < q_width + k_width)
    dimension = jnp.where(is_query, (block * q_width + offset) % HEAD, (block * k_width + offset - q_width) % HEAD)
    pair = (dimension // 2).astype(jnp.float32)
    freq = jnp.float32(500000.0) ** (-2.0 * pair / HEAD)
    angle = positions.astype(jnp.float32)[:, None] * freq[None, :]
    rotate = jnp.logical_or(is_query, is_key)[None, :]
    cosine = jnp.where(rotate, jnp.cos(angle), jnp.float32(1.0))
    sine = jnp.where(rotate, jnp.sin(angle), jnp.float32(0.0))
    return cosine[:, 0::2], sine[:, 0::2]


def reference(normed_input, positions, fixed_weight_matrix, adapter_down_map, adapter_up_map, output_gradient):
    rows, qkv = output_gradient.shape
    cosine, sine = rope_tables(positions, qkv)
    pairs = output_gradient.astype(jnp.float32).reshape(rows, qkv // 2, 2)
    first = pairs[:, :, 0] * cosine + pairs[:, :, 1] * sine
    second = pairs[:, :, 1] * cosine - pairs[:, :, 0] * sine
    unrotated_gradient = jnp.stack([first, second], axis=2).reshape(rows, qkv).astype(jnp.bfloat16)
    rank_input = jnp.dot(normed_input, adapter_down_map, preferred_element_type=jnp.float32)
    rank_gradient = jnp.dot(unrotated_gradient, adapter_up_map.T, preferred_element_type=jnp.float32)
    low_xb = rank_input.astype(jnp.bfloat16)
    rank_gradient_up = rank_gradient.astype(jnp.bfloat16)
    base = jnp.dot(unrotated_gradient, fixed_weight_matrix.T, preferred_element_type=jnp.float32)
    adapter_branch = jnp.dot(rank_gradient_up, adapter_down_map.T, preferred_element_type=jnp.float32)
    grad_x = (base + 2.0 * adapter_branch).astype(jnp.bfloat16)
    factor = 2.0 / (float(TOKENS) ** 0.5)
    grad_a = factor * jnp.dot(normed_input.T, rank_gradient_up, preferred_element_type=jnp.float32)
    grad_b = factor * jnp.dot(low_xb.T, unrotated_gradient, preferred_element_type=jnp.float32)
    return grad_x, grad_a, grad_b
```

```python
import functools
import math

import jax
import jax.numpy as jnp
from jax import lax
from jax.experimental import pallas as pl
from jax.experimental.pallas import tpu as pltpu
from jax.sharding import PartitionSpec as P

MODEL_WIDTH = 8192
KV = 1024
HEAD = 128
MESH = pl.DeviceIdType.MESH


def rope_tables(positions, width, shards, shard):
    q_width = MODEL_WIDTH // shards
    k_width = KV // shards
    lane = jnp.arange(HEAD, dtype=jnp.int32)
    pair = (lane // 2).astype(jnp.float32)
    freq = jnp.float32(500000.0) ** (-2.0 * pair / HEAD)
    angle = positions.astype(jnp.float32)[:, None] * freq[None, :]
    cosine = jnp.cos(angle)
    sine = jnp.where(lane % 2 == 0, jnp.sin(angle), -jnp.sin(angle))
    return cosine, sine


def widen(table, width, shards, shard, fill):
    q_width = MODEL_WIDTH // shards
    k_width = KV // shards
    rows = table.shape[0]
    query = jnp.tile(table, (1, q_width // HEAD))
    if k_width % HEAD == 0:
        key = jnp.tile(table, (1, k_width // HEAD))
    else:
        key = lax.dynamic_slice_in_dim(
            jnp.tile(table, (1, 2 + k_width // HEAD)), (shard * k_width) % HEAD, k_width, 1
        )
    rest = jnp.full((rows, width - q_width - k_width), fill, jnp.float32)
    return jnp.concatenate([query, key, rest], axis=1)


def unrotate(gradient, positions, shards, shard):
    rows, width = gradient.shape
    cosine, sine = rope_tables(positions, width, shards, shard)
    cosine = widen(cosine, width, shards, shard, 1.0)
    sine = widen(sine, width, shards, shard, 0.0)
    grad = gradient.astype(jnp.float32)
    even = (jnp.arange(width, dtype=jnp.int32) % 2 == 0)[None, :]
    other = jnp.where(even, jnp.roll(grad, -1, axis=1), jnp.roll(grad, 1, axis=1))
    return (grad * cosine + other * sine).astype(jnp.bfloat16)


def base_kernel(
    sizes, gy, w, out, wbuf, prx, psend, zrx, pend,
    load_sem, wsend_sem, wrecv_sem, relay_sem, psend_sem, prx_sem, zsend_sem, zrx_sem,
):
    D, K, FB, TB, NT, RS, RP = sizes
    Z = D
    N = D * K * NT
    d = lax.axis_index("dp")
    t = lax.axis_index("tensor")
    z = t // 2
    core = t % 2
    partner = t + 1 - 2 * core
    relay = D == 4
    direct = (1, 2) if relay else tuple(range(1, D))

    def owner_at(r):
        if relay:
            x = (d % 2 + r % 2) % 2
            y = (d // 2 + r // 2) % 2
            return 2 * y + x
        return (d + r) % D

    def target_of(r):
        return owner_at(r) if relay else (d + D - r) % D

    def place(ci):
        if D < 4:
            return ci // K, ci % K
        mid = ci - K
        inter = jnp.logical_and(ci >= K, ci < 3 * K)
        r = jnp.where(inter, 1 + (mid + 2 * K) % 2, ci // K)
        k = jnp.where(inter, (mid + 2 * K) // 2 - K, ci % K)
        return r, k

    barrier = pltpu.get_barrier_semaphore()
    pl.semaphore_signal(barrier, inc=1, device_id={"tensor": partner}, device_id_type=MESH)
    for r in direct:
        pl.semaphore_signal(barrier, inc=1, device_id={"dp": target_of(r)}, device_id_type=MESH)

    @pl.when(z > 0)
    def _():
        pl.semaphore_signal(barrier, inc=1, device_id={"tensor": t - 2}, device_id_type=MESH)

    @pl.when(z < Z - 1)
    def _():
        pl.semaphore_signal(barrier, inc=1, device_id={"tensor": t + 2}, device_id_type=MESH)

    loads = pltpu.make_async_copy(w, wbuf.at[0], load_sem)
    loads.start()
    ends = jnp.where(z == 0, 1, 0) + jnp.where(z == Z - 1, 1, 0)
    pl.semaphore_wait(barrier, 3 + len(direct) - ends)
    loads.wait()

    def piece(r, k):
        return wbuf.at[r, :, pl.ds(k * FB, FB), :]

    def own_copy(r, k):
        return pltpu.make_async_remote_copy(
            src_ref=piece(0, k), dst_ref=piece(r, k),
            send_sem=wsend_sem.at[r, k], recv_sem=wrecv_sem.at[r, k],
            device_id={"dp": target_of(r)}, device_id_type=MESH,
        )

    def relay_copy(r, k):
        other = 3 - r
        return pltpu.make_async_remote_copy(
            src_ref=piece(r, k), dst_ref=piece(3, k),
            send_sem=relay_sem.at[k], recv_sem=wrecv_sem.at[3, k],
            device_id={"dp": target_of(other)}, device_id_type=MESH,
        )

    for k in range(K):
        for r in direct:
            own_copy(r, k).start()

    def partner_copy(it):
        return pltpu.make_async_remote_copy(
            src_ref=psend.at[it % RS], dst_ref=prx.at[it],
            send_sem=psend_sem.at[it % RS], recv_sem=prx_sem.at[it],
            device_id={"tensor": partner}, device_id_type=MESH,
        )

    def extra_slot(j):
        r, k = place(j // NT)
        return N + k * NT + j % NT

    def line_copy(j):
        r, k = place(j // NT)
        p = owner_at(r)
        slot = jnp.where(p == z - 1, extra_slot(j), j)
        return pltpu.make_async_remote_copy(
            src_ref=prx.at[j], dst_ref=zrx.at[slot],
            send_sem=zsend_sem.at[j], recv_sem=zrx_sem.at[slot],
            device_id={"tensor": t + jnp.where(p > z, 2, -2)}, device_id_type=MESH,
        )

    def arrived(slot):
        return pltpu.make_async_copy(zrx.at[slot], zrx.at[slot], zrx_sem.at[slot])

    def produce(it):
        ci = it // NT
        tb = it % NT
        r, k = place(ci)

        @pl.when(jnp.logical_and(tb == 0, r > 0))
        def _():
            pltpu.make_async_copy(piece(r, k), piece(r, k), wrecv_sem.at[r, k]).wait()
            if relay:
                first = jnp.logical_and(r == 2, k < K // 2)
                second = jnp.logical_and(r == 1, k >= K // 2)

                @pl.when(jnp.logical_or(first, second))
                def _():
                    relay_copy(r, k).start()

        @pl.when(it >= RS)
        def _():
            partner_copy(it - RS).wait_send()

        rows = gy[pl.ds(pl.multiple_of(tb * TB, TB), TB), :]

        def half(which):
            return lax.dot_general(
                rows, wbuf[r, which, pl.ds(pl.multiple_of(k * FB, FB), FB), :],
                (((1,), (1,)), ((), ())), preferred_element_type=jnp.float32,
            )

        psend[it % RS] = half(1 - core).astype(jnp.bfloat16)
        partner_copy(it).start()
        pend[it % RP] = half(core)

    def consume(j):
        r, k = place(j // NT)
        tb = j % NT
        p = owner_at(r)
        partner_copy(j).wait_recv()
        pend[j % RP] += prx[j].astype(jnp.float32)

        @pl.when(jnp.logical_and(z <= p, z > 0))
        def _():
            arrived(j).wait()
            pend[j % RP] += zrx[j].astype(jnp.float32)

        @pl.when(jnp.logical_and(z >= p, z < Z - 1))
        def _():
            slot = jnp.where(p == z, extra_slot(j), j)
            arrived(slot).wait()
            pend[j % RP] += zrx[slot].astype(jnp.float32)

        @pl.when(p == z)
        def _():
            out[k, pl.ds(pl.multiple_of(tb * TB, TB), TB), :] = pend[j % RP]

        @pl.when(p != z)
        def _():
            prx[j] = pend[j % RP].astype(jnp.bfloat16)
            line_copy(j).start()

    def upstream(j):
        p = owner_at(place(j // NT)[0])
        low, high = z, Z - 1 - z
        return jnp.where(z < p, low, jnp.where(z > p, high, jnp.maximum(low, high)))

    @pl.loop(0, N + Z)
    def _(it):
        @pl.when(it < N)
        def _():
            produce(it)

        @pl.loop(0, Z)
        def _(u):
            j = it - 1 - u
            inside = jnp.logical_and(j >= 0, j < N)
            safe = jnp.clip(j, 0, N - 1)

            @pl.when(jnp.logical_and(inside, upstream(safe) == u))
            def _():
                consume(safe)

    for k in range(K):
        for r in direct:
            own_copy(r, k).wait_send()
        if relay:
            relay_copy(2 if k < K // 2 else 1, k).wait_send()

    @pl.loop(N - RS, N)
    def _(it):
        partner_copy(it).wait_send()

    @pl.loop(0, N)
    def _(j):
        @pl.when(owner_at(place(j // NT)[0]) != z)
        def _():
            line_copy(j).wait_send()


def base_sum(gy, w, D):
    M, cols = gy.shape
    half = w.shape[0] // 2
    FB = min(256, half)
    TB = min(512, M)
    K, NT = half // FB, M // TB
    N = D * K * NT
    RS, RP = 4, D + 1
    dma = pltpu.SemaphoreType.DMA
    out = pl.pallas_call(
        functools.partial(base_kernel, (D, K, FB, TB, NT, RS, RP)),
        out_shape=jax.ShapeDtypeStruct((K, M, FB), jnp.float32),
        in_specs=[pl.BlockSpec(memory_space=pltpu.VMEM), pl.BlockSpec(memory_space=pl.ANY)],
        out_specs=pl.BlockSpec(memory_space=pltpu.VMEM),
        scratch_shapes=[
            pltpu.VMEM((D, 2, half, cols), jnp.bfloat16),
            pltpu.VMEM((N, TB, FB), jnp.bfloat16),
            pltpu.VMEM((RS, TB, FB), jnp.bfloat16),
            pltpu.VMEM((N + K * NT, TB, FB), jnp.bfloat16),
            pltpu.VMEM((RP, TB, FB), jnp.float32),
            dma,
            dma((D, K)),
            dma((D, K)),
            dma((K,)),
            dma((RS,)),
            dma((N,)),
            dma((N,)),
            dma((N + K * NT,)),
        ],
        compiler_params=pltpu.CompilerParams(
            collective_id=0, has_side_effects=True, vmem_limit_bytes=60 * 1024 * 1024
        ),
    )(gy, w.reshape(2, half, cols))
    return out.transpose(1, 0, 2).reshape(M, half)


def on_device(
    normed_input, positions, fixed_weight_matrix, adapter_down_map, adapter_up_map, output_gradient
):
    rows, width = output_gradient.shape
    shards = lax.axis_size("tensor")
    shard = lax.axis_index("tensor")
    D = lax.axis_size("dp")
    unrotated_gradient = unrotate(output_gradient, positions, shards, shard)
    rank_input = jnp.dot(normed_input, adapter_down_map, preferred_element_type=jnp.float32)
    rank_gradient = jnp.dot(
        unrotated_gradient, adapter_up_map.T, preferred_element_type=jnp.float32
    )
    if shards == 2 * D and D & (D - 1) == 0:
        base = base_sum(unrotated_gradient, fixed_weight_matrix, D)
    else:
        terms = jnp.dot(
            unrotated_gradient,
            lax.all_gather(fixed_weight_matrix, "dp", axis=0, tiled=True).T,
            preferred_element_type=jnp.float32,
        )
        base = lax.psum_scatter(terms, "tensor", scatter_dimension=1, tiled=True)
    rank_input, rank_gradient = lax.psum((rank_input, rank_gradient), "tensor")
    low_xb = rank_input.astype(jnp.bfloat16)
    rank_gradient_up = rank_gradient.astype(jnp.bfloat16)
    factor = 2.0 / math.sqrt(rows * D)
    part_a = factor * jnp.dot(normed_input.T, rank_gradient_up, preferred_element_type=jnp.float32)
    part_b = factor * jnp.dot(low_xb.T, unrotated_gradient, preferred_element_type=jnp.float32)
    adapter_branch = jnp.dot(
        rank_gradient_up, adapter_down_map.T, preferred_element_type=jnp.float32
    )
    grad_x = (base + 2.0 * adapter_branch).astype(jnp.bfloat16)
    grad_a, grad_b = lax.psum((part_a, part_b), "dp")
    return (grad_x, grad_a, grad_b)


def solution(mesh):
    placed = (
        P("dp", "tensor"),
        P("dp"),
        P("dp", "tensor"),
        P("tensor", None),
        P(None, "tensor"),
        P("dp", "tensor"),
    )
    return jax.shard_map(
        on_device,
        mesh=mesh,
        in_specs=placed,
        out_specs=(P("dp", "tensor"), P("tensor", None), P(None, "tensor")),
        check_vma=False,
    )
```

```python
import functools
import math

import jax
import jax.numpy as jnp
from jax import lax
from jax.experimental import pallas as pl
from jax.experimental.pallas import tpu as pltpu
from jax.sharding import PartitionSpec as P

MODEL_WIDTH = 8192
KV = 1024
HEAD = 128
MESH = pl.DeviceIdType.MESH


def rope_tables(positions, width, shards, shard):
    q_width = MODEL_WIDTH // shards
    k_width = KV // shards
    lane = jnp.arange(HEAD + width - q_width, dtype=jnp.int32)
    after = lane - HEAD
    rotate = after < k_width
    dimension = jnp.where(lane < HEAD, lane, (shard * k_width + after) % HEAD)
    pair = (dimension // 2).astype(jnp.float32)
    freq = jnp.float32(500000.0) ** (-2.0 * pair / HEAD)
    angle = positions.astype(jnp.float32)[:, None] * freq[None, :]
    cosine = jnp.where(rotate, jnp.cos(angle), jnp.float32(1.0))
    sine = jnp.where(lane % 2 == 0, jnp.sin(angle), -jnp.sin(angle))
    return cosine, jnp.where(rotate, sine, jnp.float32(0.0))


def fused_kernel(
    sizes, g, cosine, sine, x, down, down_wide, up, w,
    out, out_a, out_b,
    gy, wbuf, prx, psend, zrx, pend, low_part, low_rx, low_all, low_tall, ab_own, ab_send, ab_rx,
    load_sem, wsend_sem, wrecv_sem, relay_sem, psend_sem, prx_sem, zsend_sem, zrx_sem,
    low_s1, low_r1, low_s2, low_r2, ab_s, ab_r,
):
    D, K, FB, TB, RS, RP, factor = sizes
    Z = D
    T = 2 * D
    N = D * K
    M, cols = g.shape
    F = x.shape[1]
    L = M // T
    rank = up.shape[0]
    d = lax.axis_index("dp")
    t = lax.axis_index("tensor")
    z = t // 2
    core = t % 2
    partner = t + 1 - 2 * core
    relay = D == 4
    direct = (1, 2) if relay else tuple(range(1, D))

    def owner_at(r):
        if relay:
            xx = (d % 2 + r % 2) % 2
            yy = (d // 2 + r // 2) % 2
            return 2 * yy + xx
        return (d + r) % D

    def target_of(r):
        return owner_at(r) if relay else (d + D - r) % D

    def place(ci):
        if D < 4:
            return ci // K, ci % K
        mid = ci + K
        inter = jnp.logical_and(ci >= K, ci < 3 * K)
        r = jnp.where(inter, 1 + mid % 2, ci // K)
        k = jnp.where(inter, mid // 2 - K, ci % K)
        if relay:
            last = ci % K
            k = jnp.where(ci >= 3 * K, (last % 2) * (K // 2) + last // 2, k)
        return r, k

    barrier = pltpu.get_barrier_semaphore()
    for o in range(1, T):
        pl.semaphore_signal(
            barrier, inc=1, device_id={"tensor": (t + o) % T}, device_id_type=MESH
        )
    for o in range(1, D):
        pl.semaphore_signal(barrier, inc=1, device_id={"dp": (d + o) % D}, device_id_type=MESH)
    loads = pltpu.make_async_copy(w, wbuf.at[0], load_sem)
    loads.start()
    pl.semaphore_wait(barrier, T + D - 2)
    loads.wait()

    def piece(r, k):
        return wbuf.at[r, :, pl.ds(k * FB, FB), :]

    def own_copy(r, k):
        return pltpu.make_async_remote_copy(
            src_ref=piece(0, k), dst_ref=piece(r, k),
            send_sem=wsend_sem.at[r, k], recv_sem=wrecv_sem.at[r, k],
            device_id={"dp": target_of(r)}, device_id_type=MESH,
        )

    def relay_copy(r, k):
        return pltpu.make_async_remote_copy(
            src_ref=piece(r, k), dst_ref=piece(3, k),
            send_sem=relay_sem.at[k], recv_sem=wrecv_sem.at[3, k],
            device_id={"dp": target_of(3 - r)}, device_id_type=MESH,
        )

    for k in range(K):
        for r in direct:
            own_copy(r, k).start()

    step = 128

    @pl.loop(0, M // step)
    def _(i):
        rows = pl.ds(pl.multiple_of(i * step, step), step)
        even = lax.broadcasted_iota(jnp.int32, (step, HEAD), 1) % 2 == 0
        for c in range(cols // HEAD):
            at = pl.ds(c * HEAD, HEAD)
            tab = max(0, c * HEAD - MODEL_WIDTH // T + HEAD)
            tat = pl.ds(tab, HEAD)
            val = g[rows, at].astype(jnp.float32)
            other = jnp.where(even, pltpu.roll(val, HEAD - 1, 1), pltpu.roll(val, 1, 1))
            gy[rows, at] = (val * cosine[rows, tat] + other * sine[rows, tat]).astype(jnp.bfloat16)

    nt = (((1,), (1,)), ((), ()))
    for s in range(T):
        rows = pl.ds(s * L, L)
        low_part[s, :rank] = lax.dot_general(
            down[...], x[rows, :], nt, preferred_element_type=jnp.float32
        )
        low_part[s, rank:] = lax.dot_general(
            up[...], gy[rows, :], nt, preferred_element_type=jnp.float32
        )

    def low_scatter(o):
        to = (t + o) % T
        return pltpu.make_async_remote_copy(
            src_ref=low_part.at[to], dst_ref=low_rx.at[o],
            send_sem=low_s1.at[o], recv_sem=low_r1.at[o],
            device_id={"tensor": to}, device_id_type=MESH,
        )

    def low_gather(o):
        return pltpu.make_async_remote_copy(
            src_ref=low_all.at[t], dst_ref=low_all.at[t],
            send_sem=low_s2.at[o], recv_sem=low_r2.at[o],
            device_id={"tensor": (t + o) % T}, device_id_type=MESH,
        )

    def ab_copy(o):
        return pltpu.make_async_remote_copy(
            src_ref=ab_send, dst_ref=ab_rx.at[o],
            send_sem=ab_s.at[o], recv_sem=ab_r.at[o],
            device_id={"dp": (d + o) % D}, device_id_type=MESH,
        )

    for o in range(1, T):
        low_scatter(o).start()

    def low_reduce():
        total = low_part[t]
        for o in range(1, T):
            low_scatter(o).wait_recv()
            total += low_rx[o]
        low_all[t] = total.astype(jnp.bfloat16)
        for o in range(1, T):
            low_gather(o).start()

    def low_finish():
        for o in range(1, T):
            src = (t + T - o) % T
            pltpu.make_async_copy(low_all.at[src], low_all.at[src], low_r2.at[o]).wait()
        low = jnp.concatenate([low_all[s].astype(jnp.float32) for s in range(T)], axis=1)
        low_tall[...] = low.T.astype(jnp.bfloat16)
        low = low.astype(jnp.bfloat16)
        ab_own[:, :F] = jnp.dot(low[rank:], x[...], preferred_element_type=jnp.float32)
        ab_own[:, F:] = jnp.dot(low[:rank], gy[...], preferred_element_type=jnp.float32)
        ab_send[...] = ab_own[...].astype(jnp.bfloat16)
        for o in range(1, D):
            ab_copy(o).start()

    def partner_copy(it):
        return pltpu.make_async_remote_copy(
            src_ref=psend.at[it % RS], dst_ref=prx.at[it],
            send_sem=psend_sem.at[it % RS], recv_sem=prx_sem.at[it],
            device_id={"tensor": partner}, device_id_type=MESH,
        )

    def extra_slot(j):
        return N + place(j)[1]

    def line_copy(j):
        p = owner_at(place(j)[0])
        slot = jnp.where(p == z - 1, extra_slot(j), j)
        return pltpu.make_async_remote_copy(
            src_ref=prx.at[j], dst_ref=zrx.at[slot],
            send_sem=zsend_sem.at[j], recv_sem=zrx_sem.at[slot],
            device_id={"tensor": t + jnp.where(p > z, 2, -2)}, device_id_type=MESH,
        )

    def arrived(slot):
        return pltpu.make_async_copy(zrx.at[slot], zrx.at[slot], zrx_sem.at[slot])

    def produce(it):
        r, k = place(it)

        @pl.when(r > 0)
        def _():
            pltpu.make_async_copy(piece(r, k), piece(r, k), wrecv_sem.at[r, k]).wait()
            if relay:
                first = jnp.logical_and(r == 2, k < K // 2)
                second = jnp.logical_and(r == 1, k >= K // 2)

                @pl.when(jnp.logical_or(first, second))
                def _():
                    relay_copy(r, k).start()

        @pl.when(it >= RS)
        def _():
            partner_copy(it - RS).wait_send()

        @pl.loop(0, M // TB)
        def _(tb):
            rows = pl.ds(pl.multiple_of(tb * TB, TB), TB)
            rhs = wbuf[r, :, pl.ds(pl.multiple_of(k * FB, FB), FB), :].reshape(2 * FB, cols)
            both = lax.dot_general(gy[rows, :], rhs, nt, preferred_element_type=jnp.float32)
            zero, one = both[:, :FB], both[:, FB:]
            psend[it % RS, rows, :] = jnp.where(core == 0, one, zero).astype(jnp.bfloat16)
            pend[it % RP, rows, :] = jnp.where(core == 0, zero, one)

        partner_copy(it).start()

    def consume(j):
        r, k = place(j)
        p = owner_at(r)
        partner_copy(j).wait_recv()
        pend[j % RP] += prx[j].astype(jnp.float32)

        @pl.when(jnp.logical_and(z <= p, z > 0))
        def _():
            arrived(j).wait()
            pend[j % RP] += zrx[j].astype(jnp.float32)

        @pl.when(jnp.logical_and(z >= p, z < Z - 1))
        def _():
            slot = jnp.where(p == z, extra_slot(j), j)
            arrived(slot).wait()
            pend[j % RP] += zrx[slot].astype(jnp.float32)

        @pl.when(p == z)
        def _():
            at = pl.ds(pl.multiple_of(k * FB, FB), FB)
            extra = jnp.dot(low_tall[...], down_wide[:, at], preferred_element_type=jnp.float32)
            out[:, at] = (pend[j % RP] + 2.0 * extra).astype(jnp.bfloat16)

        @pl.when(p != z)
        def _():
            prx[j] = pend[j % RP].astype(jnp.bfloat16)
            line_copy(j).start()

    def upstream(j):
        p = owner_at(place(j)[0])
        low, high = z, Z - 1 - z
        return jnp.where(z < p, low, jnp.where(z > p, high, jnp.maximum(low, high)))

    @pl.loop(0, N + Z)
    def _(it):
        @pl.when(it < N)
        def _():
            produce(it)

        @pl.when(it == 1)
        def _():
            low_reduce()

        @pl.when(it == 2)
        def _():
            low_finish()

        @pl.loop(0, Z)
        def _(u):
            j = it - 1 - u
            inside = jnp.logical_and(j >= 0, j < N)
            safe = jnp.clip(j, 0, N - 1)

            @pl.when(jnp.logical_and(inside, upstream(safe) == u))
            def _():
                consume(safe)

    for o in range(1, D):
        ab_copy(o).wait_recv()
    total = ab_own[...]
    for o in range(1, D):
        total += ab_rx[o].astype(jnp.float32)
    total = factor * total
    out_a[...] = total[:, :F]
    out_b[...] = total[:, F:]

    for o in range(1, D):
        ab_copy(o).wait_send()
    for o in range(1, T):
        low_scatter(o).wait_send()
        low_gather(o).wait_send()
    for k in range(K):
        for r in direct:
            own_copy(r, k).wait_send()
        if relay:
            relay_copy(2 if k < K // 2 else 1, k).wait_send()

    @pl.loop(N - RS, N)
    def _(it):
        partner_copy(it).wait_send()

    @pl.loop(0, N)
    def _(j):
        @pl.when(owner_at(place(j)[0]) != z)
        def _():
            line_copy(j).wait_send()


def fused(x, positions, w, down_map, up, g, D):
    M, cols = g.shape
    T = 2 * D
    half = w.shape[0] // 2
    F = x.shape[1]
    rank = up.shape[0]
    FB = 128
    TB = min(512, M)
    K = half // FB
    N = D * K
    RS, RP = 4, D + 1
    factor = 2.0 / math.sqrt(M * D)
    cosine, sine = rope_tables(positions, cols, T, lax.axis_index("tensor"))
    down = down_map.T
    down_wide = jnp.concatenate([jnp.zeros_like(down), down], axis=0)
    dma = pltpu.SemaphoreType.DMA
    vmem = pl.BlockSpec(memory_space=pltpu.VMEM)
    f32, bf16 = jnp.float32, jnp.bfloat16
    out, out_a, out_b = pl.pallas_call(
        functools.partial(fused_kernel, (D, K, FB, TB, RS, RP, factor)),
        out_shape=(
            jax.ShapeDtypeStruct((M, half), bf16),
            jax.ShapeDtypeStruct((rank, F), f32),
            jax.ShapeDtypeStruct((rank, cols), f32),
        ),
        in_specs=[vmem] * 7 + [pl.BlockSpec(memory_space=pl.ANY)],
        out_specs=(vmem, vmem, vmem),
        scratch_shapes=[
            pltpu.VMEM((M, cols), bf16),
            pltpu.VMEM((D, 2, half, cols), bf16),
            pltpu.VMEM((N, M, FB), bf16),
            pltpu.VMEM((RS, M, FB), bf16),
            pltpu.VMEM((N + K, M, FB), bf16),
            pltpu.VMEM((RP, M, FB), f32),
            pltpu.VMEM((T, 2 * rank, M // T), f32),
            pltpu.VMEM((T, 2 * rank, M // T), f32),
            pltpu.VMEM((T, 2 * rank, M // T), bf16),
            pltpu.VMEM((M, 2 * rank), bf16),
            pltpu.VMEM((rank, F + cols), f32),
            pltpu.VMEM((rank, F + cols), bf16),
            pltpu.VMEM((D, rank, F + cols), bf16),
            dma,
            dma((D, K)),
            dma((D, K)),
            dma((K,)),
            dma((RS,)),
            dma((N,)),
            dma((N,)),
            dma((N + K,)),
            dma((T,)),
            dma((T,)),
            dma((T,)),
            dma((T,)),
            dma((D,)),
            dma((D,)),
        ],
        compiler_params=pltpu.CompilerParams(
            collective_id=0, has_side_effects=True, vmem_limit_bytes=63 * 1024 * 1024
        ),
    )(g, cosine, sine, x, down, down_wide, up, w.reshape(2, half, cols))
    return out, out_a.T, out_b


def on_device(x, positions, w, down_map, up, g):
    D = lax.axis_size("dp")
    return fused(x, positions, w, down_map, up, g, D)


def solution(mesh):
    placed = (
        P("dp", "tensor"),
        P("dp"),
        P("dp", "tensor"),
        P("tensor", None),
        P(None, "tensor"),
        P("dp", "tensor"),
    )
    return jax.shard_map(
        on_device,
        mesh=mesh,
        in_specs=placed,
        out_specs=(P("dp", "tensor"), P("tensor", None), P(None, "tensor")),
        check_vma=False,
    )
```

```python
import functools
import math

import jax
import jax.numpy as jnp
from jax import lax
from jax.experimental import pallas as pl
from jax.experimental.pallas import tpu as pltpu
from jax.sharding import PartitionSpec as P

MODEL_WIDTH = 8192
KV = 1024
HEAD = 128
MESH = pl.DeviceIdType.MESH


def rope_lanes(width, shards, shard):
    q_width = MODEL_WIDTH // shards
    k_width = KV // shards
    lane = jnp.arange(HEAD + width - q_width, dtype=jnp.int32)
    after = lane - HEAD
    dimension = jnp.where(lane < HEAD, lane, (shard * k_width + after) % HEAD)
    pair = (dimension // 2).astype(jnp.float32)
    freq = jnp.float32(500000.0) ** (-2.0 * pair / HEAD)
    return freq[None, :], (after < k_width).astype(jnp.float32)[None, :]


def fused_kernel(
    sizes, g, positions, freq, rotates, x, down, down_wide, up, w,
    out, out_a, out_b,
    gy, wbuf, prx, psend, zrx, pend, fin, low_part, low_rx, low_all, low_tall, ab_own, ab_send, ab_rx,
    load_sem, wsend_sem, wrecv_sem, relay_sem, psend_sem, prx_sem, zsend_sem, zrx_sem,
    low_s1, low_r1, low_s2, low_r2, ab_s, ab_r,
):
    D, K, FB, TB, RS, RP, factor = sizes
    Z = D
    T = 2 * D
    N = D * K
    M, cols = g.shape
    F = x.shape[1]
    L = M // T
    rank = up.shape[0]
    d = lax.axis_index("dp")
    t = lax.axis_index("tensor")
    z = t // 2
    core = t % 2
    partner = t + 1 - 2 * core
    relay = D == 4
    direct = (1, 2) if relay else tuple(range(1, D))

    def owner_at(r):
        if relay:
            xx = (d % 2 + r % 2) % 2
            yy = (d // 2 + r // 2) % 2
            return 2 * yy + xx
        return (d + r) % D

    def target_of(r):
        return owner_at(r) if relay else (d + D - r) % D

    def place(ci):
        if D < 4:
            return ci // K, ci % K
        mid = ci + K
        inter = jnp.logical_and(ci >= K, ci < 3 * K)
        r = jnp.where(inter, 1 + mid % 2, ci // K)
        k = jnp.where(inter, mid // 2 - K, ci % K)
        if relay:
            last = ci % K
            k = jnp.where(ci >= 3 * K, (last % 2) * (K // 2) + last // 2, k)
        return r, k

    barrier = pltpu.get_barrier_semaphore()
    for o in range(1, T):
        pl.semaphore_signal(
            barrier, inc=1, device_id={"tensor": (t + o) % T}, device_id_type=MESH
        )
    for o in range(1, D):
        pl.semaphore_signal(barrier, inc=1, device_id={"dp": (d + o) % D}, device_id_type=MESH)
    loads = pltpu.make_async_copy(w, wbuf.at[0], load_sem)
    loads.start()
    pl.semaphore_wait(barrier, T + D - 2)

    def piece(r, k):
        return wbuf.at[r, :, pl.ds(k * FB, FB), :]

    def own_copy(r, k):
        return pltpu.make_async_remote_copy(
            src_ref=w.at[:, pl.ds(k * FB, FB), :], dst_ref=piece(r, k),
            send_sem=wsend_sem.at[r, k], recv_sem=wrecv_sem.at[r, k],
            device_id={"dp": target_of(r)}, device_id_type=MESH,
        )

    def relay_copy(r, k):
        return pltpu.make_async_remote_copy(
            src_ref=piece(r, k), dst_ref=piece(3, k),
            send_sem=relay_sem.at[k], recv_sem=wrecv_sem.at[3, k],
            device_id={"dp": target_of(3 - r)}, device_id_type=MESH,
        )

    for k in range(K):
        for r in direct:
            own_copy(r, k).start()

    step = 128
    q_width, k_width = MODEL_WIDTH // T, KV // T

    @pl.loop(0, M // step)
    def _(i):
        rows = pl.ds(pl.multiple_of(i * step, step), step)
        even = lax.broadcasted_iota(jnp.int32, (step, HEAD), 1) % 2 == 0
        place_of = jnp.broadcast_to(positions[rows, :].astype(jnp.float32), (step, HEAD))

        def table(lanes):
            angle = place_of * freq[:, lanes]
            sine = jnp.sin(angle)
            return jnp.cos(angle), jnp.where(even, sine, -sine)

        head = table(pl.ds(0, HEAD))
        for off in range(0, cols, HEAD):
            at = pl.ds(off, HEAD)
            cosine, sine = head
            if off >= q_width:
                if k_width % HEAD == 0:
                    if off >= q_width + k_width:
                        gy[rows, at] = g[rows, at]
                        continue
                else:
                    tail = pl.ds(HEAD + off - q_width, HEAD)
                    cosine, sine = table(tail)
                    turn = jnp.broadcast_to(rotates[:, tail], (step, HEAD)) > 0.5
                    cosine = jnp.where(turn, cosine, 1.0)
                    sine = jnp.where(turn, sine, 0.0)
            val = g[rows, at].astype(jnp.float32)
            other = jnp.where(even, pltpu.roll(val, HEAD - 1, 1), pltpu.roll(val, 1, 1))
            gy[rows, at] = (val * cosine + other * sine).astype(jnp.bfloat16)

    loads.wait()

    nt = (((1,), (1,)), ((), ()))
    for s in range(T):
        rows = pl.ds(s * L, L)
        low_part[s, :rank] = lax.dot_general(
            down[...], x[rows, :], nt, preferred_element_type=jnp.float32
        )
        low_part[s, rank:] = lax.dot_general(
            up[...], gy[rows, :], nt, preferred_element_type=jnp.float32
        )

    def low_scatter(o):
        to = (t + o) % T
        return pltpu.make_async_remote_copy(
            src_ref=low_part.at[to], dst_ref=low_rx.at[o],
            send_sem=low_s1.at[o], recv_sem=low_r1.at[o],
            device_id={"tensor": to}, device_id_type=MESH,
        )

    def low_gather(o):
        return pltpu.make_async_remote_copy(
            src_ref=low_all.at[t], dst_ref=low_all.at[t],
            send_sem=low_s2.at[o], recv_sem=low_r2.at[o],
            device_id={"tensor": (t + o) % T}, device_id_type=MESH,
        )

    def ab_copy(o):
        return pltpu.make_async_remote_copy(
            src_ref=ab_send, dst_ref=ab_rx.at[o],
            send_sem=ab_s.at[o], recv_sem=ab_r.at[o],
            device_id={"dp": (d + o) % D}, device_id_type=MESH,
        )

    for o in range(1, T):
        low_scatter(o).start()

    def low_reduce():
        total = low_part[t]
        for o in range(1, T):
            low_scatter(o).wait_recv()
            total += low_rx[o]
        low_all[t] = total.astype(jnp.bfloat16)
        for o in range(1, T):
            low_gather(o).start()

    def low_finish():
        for o in range(1, T):
            src = (t + T - o) % T
            pltpu.make_async_copy(low_all.at[src], low_all.at[src], low_r2.at[o]).wait()
        low = jnp.concatenate([low_all[s].astype(jnp.float32) for s in range(T)], axis=1)
        low_tall[...] = low.T.astype(jnp.bfloat16)
        low = low.astype(jnp.bfloat16)
        ab_own[:, :F] = jnp.dot(low[rank:], x[...], preferred_element_type=jnp.float32)
        ab_own[:, F:] = jnp.dot(low[:rank], gy[...], preferred_element_type=jnp.float32)
        ab_send[...] = ab_own[...].astype(jnp.bfloat16)
        for o in range(1, D):
            ab_copy(o).start()

    def partner_copy(it):
        return pltpu.make_async_remote_copy(
            src_ref=psend.at[it % RS], dst_ref=prx.at[it],
            send_sem=psend_sem.at[it % RS], recv_sem=prx_sem.at[it],
            device_id={"tensor": partner}, device_id_type=MESH,
        )

    def extra_slot(j):
        return N + place(j)[1]

    def line_copy(j):
        p = owner_at(place(j)[0])
        slot = jnp.where(p == z - 1, extra_slot(j), j)
        return pltpu.make_async_remote_copy(
            src_ref=prx.at[j], dst_ref=zrx.at[slot],
            send_sem=zsend_sem.at[j], recv_sem=zrx_sem.at[slot],
            device_id={"tensor": t + jnp.where(p > z, 2, -2)}, device_id_type=MESH,
        )

    def arrived(slot):
        return pltpu.make_async_copy(zrx.at[slot], zrx.at[slot], zrx_sem.at[slot])

    def produce(it):
        r, k = place(it)

        @pl.when(r > 0)
        def _():
            pltpu.make_async_copy(piece(r, k), piece(r, k), wrecv_sem.at[r, k]).wait()
            if relay:
                first = jnp.logical_and(r == 2, k < K // 2)
                second = jnp.logical_and(r == 1, k >= K // 2)

                @pl.when(jnp.logical_or(first, second))
                def _():
                    relay_copy(r, k).start()

        @pl.when(it >= RS)
        def _():
            partner_copy(it - RS).wait_send()

        @pl.loop(0, M // TB)
        def _(tb):
            rows = pl.ds(pl.multiple_of(tb * TB, TB), TB)
            rhs = wbuf[r, :, pl.ds(pl.multiple_of(k * FB, FB), FB), :].reshape(2 * FB, cols)
            both = lax.dot_general(gy[rows, :], rhs, nt, preferred_element_type=jnp.float32)
            zero, one = both[:, :FB], both[:, FB:]
            psend[it % RS, rows, :] = jnp.where(core == 0, one, zero).astype(jnp.bfloat16)
            pend[it % RP, rows, :] = jnp.where(core == 0, zero, one)

        partner_copy(it).start()

    def forward(j):
        r, k = place(j)
        p = owner_at(r)
        partner_copy(j).wait_recv()
        pend[j % RP] += prx[j].astype(jnp.float32)

        @pl.when(jnp.logical_and(z < p, z > 0))
        def _():
            arrived(j).wait()
            pend[j % RP] += zrx[j].astype(jnp.float32)

        @pl.when(jnp.logical_and(z > p, z < Z - 1))
        def _():
            arrived(j).wait()
            pend[j % RP] += zrx[j].astype(jnp.float32)

        @pl.when(p == z)
        def _():
            fin[k] = pend[j % RP]

        @pl.when(p != z)
        def _():
            prx[j] = pend[j % RP].astype(jnp.bfloat16)
            line_copy(j).start()

    def finish(j):
        k = place(j)[1]
        at = pl.ds(pl.multiple_of(k * FB, FB), FB)

        @pl.when(z > 0)
        def _():
            arrived(j).wait()
            fin[k] += zrx[j].astype(jnp.float32)

        @pl.when(z < Z - 1)
        def _():
            arrived(N + k).wait()
            fin[k] += zrx[N + k].astype(jnp.float32)

        extra = jnp.dot(low_tall[...], down_wide[:, at], preferred_element_type=jnp.float32)
        out[:, at] = (fin[k] + 2.0 * extra).astype(jnp.bfloat16)

    def upstream(j):
        p = owner_at(place(j)[0])
        return jnp.where(z < p, z, jnp.where(z > p, Z - 1 - z, 0))

    @pl.loop(0, N + Z)
    def _(it):
        @pl.loop(0, Z)
        def _(u):
            j = it - 1 - u
            inside = jnp.logical_and(j >= 0, j < N)
            safe = jnp.clip(j, 0, N - 1)

            @pl.when(jnp.logical_and(inside, upstream(safe) == u))
            def _():
                forward(safe)

        @pl.when(it < N)
        def _():
            produce(it)

        @pl.when(it == 1)
        def _():
            low_reduce()

        @pl.when(it == 2)
        def _():
            low_finish()

        @pl.loop(0, 2)
        def _(end):
            j = it - jnp.where(end == 1, Z, Z + K)
            inside = jnp.logical_and(
                jnp.logical_and(j >= 0, j < N), (j >= N - K) == (end == 1)
            )
            safe = jnp.clip(j, 0, N - 1)

            @pl.when(jnp.logical_and(inside, owner_at(place(safe)[0]) == z))
            def _():
                finish(safe)

    for o in range(1, D):
        ab_copy(o).wait_recv()
    total = ab_own[...]
    for o in range(1, D):
        total += ab_rx[o].astype(jnp.float32)
    total = factor * total
    out_a[...] = total[:, :F]
    out_b[...] = total[:, F:]

    for o in range(1, D):
        ab_copy(o).wait_send()
    for o in range(1, T):
        low_scatter(o).wait_send()
        low_gather(o).wait_send()
    for k in range(K):
        for r in direct:
            own_copy(r, k).wait_send()
        if relay:
            relay_copy(2 if k < K // 2 else 1, k).wait_send()

    @pl.loop(N - RS, N)
    def _(it):
        partner_copy(it).wait_send()

    @pl.loop(0, N)
    def _(j):
        @pl.when(owner_at(place(j)[0]) != z)
        def _():
            line_copy(j).wait_send()


def fused(x, positions, w, down_map, up, g, D):
    M, cols = g.shape
    T = 2 * D
    half = w.shape[0] // 2
    F = x.shape[1]
    rank = up.shape[0]
    FB = 128
    TB = min(512, M)
    K = half // FB
    N = D * K
    RS, RP = 4, D
    factor = 2.0 / math.sqrt(M * D)
    freq, rotates = rope_lanes(cols, T, lax.axis_index("tensor"))
    down = down_map.T
    down_wide = jnp.concatenate([jnp.zeros_like(down), down], axis=0)
    dma = pltpu.SemaphoreType.DMA
    vmem = pl.BlockSpec(memory_space=pltpu.VMEM)
    f32, bf16 = jnp.float32, jnp.bfloat16
    out, out_a, out_b = pl.pallas_call(
        functools.partial(fused_kernel, (D, K, FB, TB, RS, RP, factor)),
        out_shape=(
            jax.ShapeDtypeStruct((M, half), bf16),
            jax.ShapeDtypeStruct((rank, F), f32),
            jax.ShapeDtypeStruct((rank, cols), f32),
        ),
        in_specs=[vmem] * 8 + [pl.BlockSpec(memory_space=pl.ANY)],
        out_specs=(vmem, vmem, vmem),
        scratch_shapes=[
            pltpu.VMEM((M, cols), bf16),
            pltpu.VMEM((D, 2, half, cols), bf16),
            pltpu.VMEM((N, M, FB), bf16),
            pltpu.VMEM((RS, M, FB), bf16),
            pltpu.VMEM((N + K, M, FB), bf16),
            pltpu.VMEM((RP, M, FB), f32),
            pltpu.VMEM((K, M, FB), f32),
            pltpu.VMEM((T, 2 * rank, M // T), f32),
            pltpu.VMEM((T, 2 * rank, M // T), f32),
            pltpu.VMEM((T, 2 * rank, M // T), bf16),
            pltpu.VMEM((M, 2 * rank), bf16),
            pltpu.VMEM((rank, F + cols), f32),
            pltpu.VMEM((rank, F + cols), bf16),
            pltpu.VMEM((D, rank, F + cols), bf16),
            dma,
            dma((D, K)),
            dma((D, K)),
            dma((K,)),
            dma((RS,)),
            dma((N,)),
            dma((N,)),
            dma((N + K,)),
            dma((T,)),
            dma((T,)),
            dma((T,)),
            dma((T,)),
            dma((D,)),
            dma((D,)),
        ],
        compiler_params=pltpu.CompilerParams(
            collective_id=0, has_side_effects=True, vmem_limit_bytes=63 * 1024 * 1024
        ),
    )(g, positions[:, None], freq, rotates, x, down, down_wide, up, w.reshape(2, half, cols))
    return out, out_a.T, out_b


def on_device(x, positions, w, down_map, up, g):
    D = lax.axis_size("dp")
    return fused(x, positions, w, down_map, up, g, D)


def solution(mesh):
    placed = (
        P("dp", "tensor"),
        P("dp"),
        P("dp", "tensor"),
        P("tensor", None),
        P(None, "tensor"),
        P("dp", "tensor"),
    )
    return jax.shard_map(
        on_device,
        mesh=mesh,
        in_specs=placed,
        out_specs=(P("dp", "tensor"), P("tensor", None), P(None, "tensor")),
        check_vma=False,
    )
```

```python
import functools
import math

import jax
import jax.numpy as jnp
from jax import lax
from jax.experimental import pallas as pl
from jax.experimental.pallas import tpu as pltpu
from jax.sharding import PartitionSpec as P

MODEL_WIDTH = 8192
KV = 1024
HEAD = 128
MESH = pl.DeviceIdType.MESH


def rope_lanes(width, shards, shard):
    q_width = MODEL_WIDTH // shards
    k_width = KV // shards
    lane = jnp.arange(HEAD + width - q_width, dtype=jnp.int32)
    after = lane - HEAD
    dimension = jnp.where(lane < HEAD, lane, (shard * k_width + after) % HEAD)
    pair = (dimension // 2).astype(jnp.float32)
    freq = jnp.float32(500000.0) ** (-2.0 * pair / HEAD)
    return freq[None, :], (after < k_width).astype(jnp.float32)[None, :]


def fused_kernel(
    sizes, g, positions, freq, rotates, x, down, down_wide, up, w,
    out, out_a, out_b,
    gy, wbuf, prx, psend, zrx, pend, fin, low_part, low_rx, low_all, low_tall, ab_own, ab_send, ab_rx,
    load_sem, wsend_sem, wrecv_sem, relay_sem, psend_sem, prx_sem, zsend_sem, zrx_sem,
    low_s1, low_r1, low_s2, low_r2, ab_s, ab_r,
):
    D, K, FB, TB, S, RS, RP, factor = sizes
    Z = D
    T = 2 * D
    N = D * K
    M, cols = g.shape
    F = x.shape[1]
    L = M // T
    rank = up.shape[0]
    d = lax.axis_index("dp")
    t = lax.axis_index("tensor")
    z = t // 2
    core = t % 2
    partner = t + 1 - 2 * core
    relay = D == 4
    direct = (1, 2) if relay else tuple(range(1, D))

    def owner_at(r):
        if relay:
            xx = (d % 2 + r % 2) % 2
            yy = (d // 2 + r // 2) % 2
            return 2 * yy + xx
        return (d + r) % D

    def target_of(r):
        return owner_at(r) if relay else (d + D - r) % D

    def place(ci):
        if D < 4:
            return ci // K, ci % K
        mid = ci + K
        inter = jnp.logical_and(ci >= K, ci < 3 * K)
        r = jnp.where(inter, 1 + mid % 2, ci // K)
        k = jnp.where(inter, mid // 2 - K, ci % K)
        if relay:
            last = ci % K
            k = jnp.where(ci >= 3 * K, (last % 2) * (K // 2) + last // 2, k)
        return r, k

    barrier = pltpu.get_barrier_semaphore()
    for o in range(1, T):
        pl.semaphore_signal(
            barrier, inc=1, device_id={"tensor": (t + o) % T}, device_id_type=MESH
        )
    for o in range(1, D):
        pl.semaphore_signal(barrier, inc=1, device_id={"dp": (d + o) % D}, device_id_type=MESH)
    loads = pltpu.make_async_copy(w, wbuf.at[0], load_sem)
    loads.start()
    pl.semaphore_wait(barrier, T + D - 2)

    def piece(r, k):
        return wbuf.at[r, :, pl.ds(k * FB, FB), :]

    def own_copy(r, k):
        return pltpu.make_async_remote_copy(
            src_ref=w.at[:, pl.ds(k * FB, FB), :], dst_ref=piece(r, k),
            send_sem=wsend_sem.at[r, k], recv_sem=wrecv_sem.at[r, k],
            device_id={"dp": target_of(r)}, device_id_type=MESH,
        )

    def relay_copy(r, k):
        return pltpu.make_async_remote_copy(
            src_ref=piece(r, k), dst_ref=piece(3, k),
            send_sem=relay_sem.at[k], recv_sem=wrecv_sem.at[3, k],
            device_id={"dp": target_of(3 - r)}, device_id_type=MESH,
        )

    for k in range(K):
        for r in direct:
            own_copy(r, k).start()

    step = 128
    q_width, k_width = MODEL_WIDTH // T, KV // T

    @pl.loop(0, M // step)
    def _(i):
        rows = pl.ds(pl.multiple_of(i * step, step), step)
        even = lax.broadcasted_iota(jnp.int32, (step, HEAD), 1) % 2 == 0
        place_of = jnp.broadcast_to(positions[rows, :].astype(jnp.float32), (step, HEAD))

        def table(lanes):
            angle = place_of * freq[:, lanes]
            sine = jnp.sin(angle)
            return jnp.cos(angle), jnp.where(even, sine, -sine)

        head = table(pl.ds(0, HEAD))
        for off in range(0, cols, HEAD):
            at = pl.ds(off, HEAD)
            cosine, sine = head
            if off >= q_width:
                if k_width % HEAD == 0:
                    if off >= q_width + k_width:
                        gy[rows, at] = g[rows, at]
                        continue
                else:
                    tail = pl.ds(HEAD + off - q_width, HEAD)
                    cosine, sine = table(tail)
                    turn = jnp.broadcast_to(rotates[:, tail], (step, HEAD)) > 0.5
                    cosine = jnp.where(turn, cosine, 1.0)
                    sine = jnp.where(turn, sine, 0.0)
            val = g[rows, at].astype(jnp.float32)
            other = jnp.where(even, pltpu.roll(val, HEAD - 1, 1), pltpu.roll(val, 1, 1))
            gy[rows, at] = (val * cosine + other * sine).astype(jnp.bfloat16)

    loads.wait()

    nt = (((1,), (1,)), ((), ()))
    for s in range(T):
        rows = pl.ds(s * L, L)
        low_part[s, :rank] = lax.dot_general(
            down[...], x[rows, :], nt, preferred_element_type=jnp.float32
        )
        low_part[s, rank:] = lax.dot_general(
            up[...], gy[rows, :], nt, preferred_element_type=jnp.float32
        )

    def low_scatter(o):
        to = (t + o) % T
        return pltpu.make_async_remote_copy(
            src_ref=low_part.at[to], dst_ref=low_rx.at[o],
            send_sem=low_s1.at[o], recv_sem=low_r1.at[o],
            device_id={"tensor": to}, device_id_type=MESH,
        )

    def low_gather(o):
        return pltpu.make_async_remote_copy(
            src_ref=low_all.at[t], dst_ref=low_all.at[t],
            send_sem=low_s2.at[o], recv_sem=low_r2.at[o],
            device_id={"tensor": (t + o) % T}, device_id_type=MESH,
        )

    def ab_copy(o):
        return pltpu.make_async_remote_copy(
            src_ref=ab_send, dst_ref=ab_rx.at[o],
            send_sem=ab_s.at[o], recv_sem=ab_r.at[o],
            device_id={"dp": (d + o) % D}, device_id_type=MESH,
        )

    for o in range(1, T):
        low_scatter(o).start()

    def low_reduce():
        total = low_part[t]
        for o in range(1, T):
            low_scatter(o).wait_recv()
            total += low_rx[o]
        low_all[t] = total.astype(jnp.bfloat16)
        for o in range(1, T):
            low_gather(o).start()

    def low_finish():
        for o in range(1, T):
            src = (t + T - o) % T
            pltpu.make_async_copy(low_all.at[src], low_all.at[src], low_r2.at[o]).wait()
        low = jnp.concatenate([low_all[s].astype(jnp.float32) for s in range(T)], axis=1)
        low_tall[...] = low.T.astype(jnp.bfloat16)
        low = low.astype(jnp.bfloat16)
        ab_own[:, :F] = jnp.dot(low[rank:], x[...], preferred_element_type=jnp.float32)
        ab_own[:, F:] = jnp.dot(low[:rank], gy[...], preferred_element_type=jnp.float32)
        ab_send[...] = ab_own[...].astype(jnp.bfloat16)
        for o in range(1, D):
            ab_copy(o).start()

    def partner_copy(it):
        return pltpu.make_async_remote_copy(
            src_ref=psend.at[it % RS], dst_ref=prx.at[it],
            send_sem=psend_sem.at[it % RS], recv_sem=prx_sem.at[it],
            device_id={"tensor": partner}, device_id_type=MESH,
        )

    def extra_slot(j):
        return N + place(j)[1]

    def part(q):
        return pl.ds(pl.multiple_of(q * (M // S), M // S), M // S)

    def line_copy(j, q):
        p = owner_at(place(j)[0])
        slot = jnp.where(p == z - 1, extra_slot(j), j)
        return pltpu.make_async_remote_copy(
            src_ref=prx.at[j, part(q), :], dst_ref=zrx.at[slot, part(q), :],
            send_sem=zsend_sem.at[j, q], recv_sem=zrx_sem.at[slot, q],
            device_id={"tensor": t + jnp.where(p > z, 2, -2)}, device_id_type=MESH,
        )

    def arrived(slot, q):
        block = zrx.at[slot, part(q), :]
        return pltpu.make_async_copy(block, block, zrx_sem.at[slot, q])

    def produce(it):
        r, k = place(it)

        @pl.when(r > 0)
        def _():
            pltpu.make_async_copy(piece(r, k), piece(r, k), wrecv_sem.at[r, k]).wait()
            if relay:
                first = jnp.logical_and(r == 2, k < K // 2)
                second = jnp.logical_and(r == 1, k >= K // 2)

                @pl.when(jnp.logical_or(first, second))
                def _():
                    relay_copy(r, k).start()

        @pl.when(it >= RS)
        def _():
            partner_copy(it - RS).wait_send()

        @pl.loop(0, M // TB)
        def _(tb):
            rows = pl.ds(pl.multiple_of(tb * TB, TB), TB)
            rhs = wbuf[r, :, pl.ds(pl.multiple_of(k * FB, FB), FB), :].reshape(2 * FB, cols)
            both = lax.dot_general(gy[rows, :], rhs, nt, preferred_element_type=jnp.float32)
            zero, one = both[:, :FB], both[:, FB:]
            psend[it % RS, rows, :] = jnp.where(core == 0, one, zero).astype(jnp.bfloat16)
            pend[it % RP, rows, :] = jnp.where(core == 0, zero, one)

        partner_copy(it).start()

    def forward(j):
        r, k = place(j)
        p = owner_at(r)
        partner_copy(j).wait_recv()
        inner = jnp.logical_or(
            jnp.logical_and(z < p, z > 0), jnp.logical_and(z > p, z < Z - 1)
        )

        @pl.when(p == z)
        def _():
            fin[k] = pend[j % RP] + prx[j].astype(jnp.float32)

        @pl.when(p != z)
        def _():
            @pl.loop(0, S)
            def _(q):
                rows = part(q)
                pend[j % RP, rows, :] += prx[j, rows, :].astype(jnp.float32)

                @pl.when(inner)
                def _():
                    arrived(j, q).wait()
                    pend[j % RP, rows, :] += zrx[j, rows, :].astype(jnp.float32)

                prx[j, rows, :] = pend[j % RP, rows, :].astype(jnp.bfloat16)
                line_copy(j, q).start()

    def finish(j):
        k = place(j)[1]
        at = pl.ds(pl.multiple_of(k * FB, FB), FB)

        @pl.loop(0, S)
        def _(q):
            rows = part(q)

            @pl.when(z > 0)
            def _():
                arrived(j, q).wait()
                fin[k, rows, :] += zrx[j, rows, :].astype(jnp.float32)

            @pl.when(z < Z - 1)
            def _():
                arrived(N + k, q).wait()
                fin[k, rows, :] += zrx[N + k, rows, :].astype(jnp.float32)

            extra = jnp.dot(
                low_tall[rows, :], down_wide[:, at], preferred_element_type=jnp.float32
            )
            out[rows, at] = (fin[k, rows, :] + 2.0 * extra).astype(jnp.bfloat16)

    def upstream(j):
        p = owner_at(place(j)[0])
        return jnp.where(z < p, z, jnp.where(z > p, Z - 1 - z, 0))

    @pl.loop(0, N + Z)
    def _(it):
        @pl.loop(0, Z)
        def _(u):
            j = it - 1 - u
            inside = jnp.logical_and(j >= 0, j < N)
            safe = jnp.clip(j, 0, N - 1)

            @pl.when(jnp.logical_and(inside, upstream(safe) == u))
            def _():
                forward(safe)

        @pl.when(it < N)
        def _():
            produce(it)

        @pl.when(it == 1)
        def _():
            low_reduce()

        @pl.when(it == 2)
        def _():
            low_finish()

        @pl.loop(0, 2)
        def _(end):
            j = it - jnp.where(end == 1, Z, Z + K)
            inside = jnp.logical_and(
                jnp.logical_and(j >= 0, j < N), (j >= N - K) == (end == 1)
            )
            safe = jnp.clip(j, 0, N - 1)

            @pl.when(jnp.logical_and(inside, owner_at(place(safe)[0]) == z))
            def _():
                finish(safe)

    for o in range(1, D):
        ab_copy(o).wait_recv()
    total = ab_own[...]
    for o in range(1, D):
        total += ab_rx[o].astype(jnp.float32)
    total = factor * total
    out_a[...] = total[:, :F]
    out_b[...] = total[:, F:]

    for o in range(1, D):
        ab_copy(o).wait_send()
    for o in range(1, T):
        low_scatter(o).wait_send()
        low_gather(o).wait_send()
    for k in range(K):
        for r in direct:
            own_copy(r, k).wait_send()
        if relay:
            relay_copy(2 if k < K // 2 else 1, k).wait_send()

    @pl.loop(N - RS, N)
    def _(it):
        partner_copy(it).wait_send()

    @pl.loop(0, N)
    def _(j):
        @pl.when(owner_at(place(j)[0]) != z)
        def _():
            for q in range(S):
                line_copy(j, q).wait_send()


def fused(x, positions, w, down_map, up, g, D):
    M, cols = g.shape
    T = 2 * D
    half = w.shape[0] // 2
    F = x.shape[1]
    rank = up.shape[0]
    FB = 128
    TB = min(512, M)
    K = half // FB
    N = D * K
    S, RS, RP = 4, 4, D
    factor = 2.0 / math.sqrt(M * D)
    freq, rotates = rope_lanes(cols, T, lax.axis_index("tensor"))
    down = down_map.T
    down_wide = jnp.concatenate([jnp.zeros_like(down), down], axis=0)
    dma = pltpu.SemaphoreType.DMA
    vmem = pl.BlockSpec(memory_space=pltpu.VMEM)
    f32, bf16 = jnp.float32, jnp.bfloat16
    out, out_a, out_b = pl.pallas_call(
        functools.partial(fused_kernel, (D, K, FB, TB, S, RS, RP, factor)),
        out_shape=(
            jax.ShapeDtypeStruct((M, half), bf16),
            jax.ShapeDtypeStruct((rank, F), f32),
            jax.ShapeDtypeStruct((rank, cols), f32),
        ),
        in_specs=[vmem] * 8 + [pl.BlockSpec(memory_space=pl.ANY)],
        out_specs=(vmem, vmem, vmem),
        scratch_shapes=[
            pltpu.VMEM((M, cols), bf16),
            pltpu.VMEM((D, 2, half, cols), bf16),
            pltpu.VMEM((N, M, FB), bf16),
            pltpu.VMEM((RS, M, FB), bf16),
            pltpu.VMEM((N + K, M, FB), bf16),
            pltpu.VMEM((RP, M, FB), f32),
            pltpu.VMEM((K, M, FB), f32),
            pltpu.VMEM((T, 2 * rank, M // T), f32),
            pltpu.VMEM((T, 2 * rank, M // T), f32),
            pltpu.VMEM((T, 2 * rank, M // T), bf16),
            pltpu.VMEM((M, 2 * rank), bf16),
            pltpu.VMEM((rank, F + cols), f32),
            pltpu.VMEM((rank, F + cols), bf16),
            pltpu.VMEM((D, rank, F + cols), bf16),
            dma,
            dma((D, K)),
            dma((D, K)),
            dma((K,)),
            dma((RS,)),
            dma((N,)),
            dma((N, S)),
            dma((N + K, S)),
            dma((T,)),
            dma((T,)),
            dma((T,)),
            dma((T,)),
            dma((D,)),
            dma((D,)),
        ],
        compiler_params=pltpu.CompilerParams(
            collective_id=0, has_side_effects=True, vmem_limit_bytes=63 * 1024 * 1024
        ),
    )(g, positions[:, None], freq, rotates, x, down, down_wide, up, w.reshape(2, half, cols))
    return out, out_a.T, out_b


def on_device(x, positions, w, down_map, up, g):
    D = lax.axis_size("dp")
    return fused(x, positions, w, down_map, up, g, D)


def solution(mesh):
    placed = (
        P("dp", "tensor"),
        P("dp"),
        P("dp", "tensor"),
        P("tensor", None),
        P(None, "tensor"),
        P("dp", "tensor"),
    )
    return jax.shard_map(
        on_device,
        mesh=mesh,
        in_specs=placed,
        out_specs=(P("dp", "tensor"), P("tensor", None), P(None, "tensor")),
        check_vma=False,
    )
```
